1024 devices in a mesh: sec: 32 (over x, z_lo, core), row: 4 (over z_hi), col: 8 (over y).
Axes of the slice: x: 8, y: 8, z: 8 (z_hi: 4, z_lo: 2; z = z_hi * 2 + z_lo), core: 2. Of those that a mesh axis runs over, the one named last changes fastest.
Arguments:
- amplitudes: bfloat16 [32, 2, 512, 8192], P('sec', None, 'row', 'col'), may hold values from -0.25 to 0.25, as said below
- state_energies: float32 [32, 8192], P('sec', 'col'), may hold values from 1.25 to 12
- radii_table: int32 [33], replicated, may hold values from 20 to 532, as said below
- plan: int32 [32, 2], P('sec'), may hold values from 0 to 31, as said below
- entry_r: float32 [32, 512, 512], P('sec', 'col', 'row'), may hold values from -16 to 48, as said below
- fresh_r: float32 [1, 512, 512], P(None, 'col', 'row'), may hold values from -16 to 48, as said below
Outputs:
- exit_r: float32 [2, 32, 512, 512], P(None, 'sec', 'col', 'row')
The draws below stay inside these ranges and needn't reach their ends.
Inputs may be any that keep to these rules, and one draw needn't show every extreme that they name: Each sector's outer-boundary amplitudes are correlated with its inner-boundary ones. `radii_table`: strictly increasing; consecutive radii differ by 4 to 16; the first is at least 20 and the last equals 532. plan[s, t] equals plan[s-1, t-1] for s, t >= 1. `entry_r`: symmetric positive definite, every eigenvalue at least 0.5. `fresh_r`: symmetric positive definite, every eigenvalue at least 0.5.
All inputs are finite; a program needn't handle non-finite values.
Results may differ from the reference program's by a relative error of at most 0.0016.
Values may be sent and summed in bfloat16 or wider, within the bound.
No kernel may reach another device: no remote copies, remote signals or barrier semaphores. Data moves between devices by JAX's collectives and lax.ppermute only.
A program may use at most 32 MiB of HBM per device.

```python
import math
import jax
import jax.numpy as jnp
from jax import lax

N = 512
K = 8192
ENERGIES = 32
TICKS = 2
SECTORS = 32


def channel_mixer(key):
    key_left, key_right, key_gain = jax.random.split(key, 3)
    identity = jnp.eye(N, dtype=jnp.float32)
    left = identity + 0.35 * jnp.clip(jax.random.normal(key_left, (N, N), jnp.float32), -5.0, 5.0) / math.sqrt(N)
    right = identity + 0.35 * jnp.clip(jax.random.normal(key_right, (N, N), jnp.float32), -5.0, 5.0) / math.sqrt(N)
    gains = jnp.exp(jax.random.uniform(key_gain, (N,), jnp.float32, math.log(0.5), math.log(4.0)))
    return jnp.dot(left * gains[None, :], right, precision=lax.Precision.HIGHEST)


def draw_amplitudes(key, part):
    base = jax.random.fold_in(key, 11)
    key_inner = jax.random.fold_in(base, 0)
    key_other = jax.random.fold_in(base, 1)
    key_mix = jax.random.fold_in(base, 3)
    mixer = channel_mixer(key_mix)
    inner = jnp.clip(jax.random.normal(key_inner, (SECTORS, N, K), jnp.float32), -5.0, 5.0)
    other = jnp.clip(jax.random.normal(key_other, (SECTORS, N, K), jnp.float32), -5.0, 5.0)
    inner = jnp.einsum('nm,smk->snk', mixer, inner, precision=lax.Precision.HIGHEST)
    other = jnp.einsum('nm,smk->snk', mixer, other, precision=lax.Precision.HIGHEST)
    outer = 0.8 * inner + 0.6 * other
    stacked = jnp.stack([inner, outer], 1) / math.sqrt(K)
    return jnp.clip(stacked, -0.25, 0.25).astype(jnp.bfloat16)


def draw_radii_table(key, part):
    base = jax.random.fold_in(key, 23)
    widths = jax.random.randint(base, (SECTORS,), 4, 17, jnp.int32)
    outermost = 20 + 16 * SECTORS
    first = outermost - jnp.sum(widths)
    table = jnp.concatenate([first[None], first + jnp.cumsum(widths)])
    return table.astype(jnp.int32)


def draw_plan(key, part):
    base = jax.random.fold_in(key, 31)
    stream = jax.random.randint(base, (SECTORS + TICKS - 1,), 0, ENERGIES, jnp.int32)
    stream = stream.at[0].set(0)
    stream = stream.at[SECTORS + TICKS - 2].set(ENERGIES - 1)
    sector_ids = jnp.arange(SECTORS, dtype=jnp.int32)[:, None]
    period_ids = jnp.arange(TICKS, dtype=jnp.int32)[None, :]
    return stream[period_ids - sector_ids + SECTORS - 1].astype(jnp.int32)


def definite_matrices(key, count):
    key_base = jax.random.fold_in(key, 0)
    key_spread = jax.random.fold_in(key, 2)
    values = jnp.clip(jax.random.normal(key_base, (count, N, N), jnp.float32), -5.0, 5.0)
    spread = jnp.exp(jax.random.uniform(key_spread, (count, 1, N), jnp.float32, math.log(0.05), math.log(20.0)))
    gram = jnp.einsum('snm,skm->snk', values * spread, values, precision=lax.Precision.HIGHEST) / N
    gram = 0.5 * (gram + jnp.swapaxes(gram, 1, 2))
    return 0.5 * jnp.eye(N, dtype=jnp.float32)[None] + gram


def draw_entry_r(key, part):
    return definite_matrices(jax.random.fold_in(key, 41), SECTORS)


def draw_fresh_r(key, part):
    return definite_matrices(jax.random.fold_in(key, 43), TICKS - 1)


def level_of(stream_key, extent, cuts, smallest, largest):
    level = 1.0
    for position, parts in cuts:
        draws = jax.random.uniform(jax.random.fold_in(jax.random.fold_in(stream_key, 6), position), (parts,), jnp.float32, smallest / len(cuts), largest / len(cuts))
        level = level * jnp.repeat(jnp.exp(draws), extent[position] // parts).reshape((-1,) + (1,) * (len(extent) - 1 - position))
    return level


def setup_inputs(seed: int = 0) -> dict:
    arg_keys = jax.random.split(jax.random.key(seed), 7)
    amplitudes = draw_amplitudes(jax.random.fold_in(arg_keys[6], 71), 0)
    state_energies = jnp.clip(jnp.exp(math.log(12.0) - 2.261763 * jax.random.uniform(arg_keys[1], (SECTORS, K), jnp.float32) ** level_of(arg_keys[1], (SECTORS, K), ((0, 32), (1, 8)), -0.2, 0.2)), 1.25, 12.0)
    radii_table = draw_radii_table(jax.random.fold_in(arg_keys[6], 71), 0)
    plan = draw_plan(jax.random.fold_in(arg_keys[6], 71), 0)
    entry_r = draw_entry_r(jax.random.fold_in(arg_keys[6], 71), 0)
    fresh_r = draw_fresh_r(jax.random.fold_in(arg_keys[6], 71), 0)
    return {"amplitudes": amplitudes, "state_energies": state_energies, "radii_table": radii_table, "plan": plan, "entry_r": entry_r, "fresh_r": fresh_r}


def sector_pass(panels, levels, sector_width, energy, entering):
    weight = 8.0 / (sector_width * (levels - energy))
    scaled = (panels.astype(jnp.float32) * weight).astype(jnp.bfloat16)
    green_ll = jnp.dot(scaled[0].astype(jnp.float32), panels[0].T.astype(jnp.float32), preferred_element_type=jnp.float32)
    green_lr = jnp.dot(scaled[0].astype(jnp.float32), panels[1].T.astype(jnp.float32), preferred_element_type=jnp.float32)
    green_rr = jnp.dot(scaled[1].astype(jnp.float32), panels[1].T.astype(jnp.float32), preferred_element_type=jnp.float32)
    factor = jnp.linalg.cholesky(green_ll + entering)
    solved = jax.scipy.linalg.solve_triangular(factor, green_lr, lower=True)
    return green_rr - jnp.dot(solved.T, solved, precision=lax.Precision.HIGHEST)

def sector_items(items):
    return sector_pass(items[0], items[1], items[2], items[3], items[4])

def reference(amplitudes, state_energies, radii_table, plan, entry_r, fresh_r):
    widths = (radii_table[1:] - radii_table[:-1]).astype(jnp.float32)
    current = entry_r
    results = []
    for period in range(TICKS):
        energies = plan[:, period].astype(jnp.float32) / ENERGIES
        produced = lax.map(sector_items, (amplitudes, state_energies, widths, energies, current))
        results.append(produced)
        if period + 1 < TICKS:
            current = jnp.concatenate([fresh_r[period][None], produced[:-1]], 0)
    return jnp.stack(results, 0)
```

```python
import jax
import jax.numpy as jnp
from jax import lax
from jax.experimental import pallas as pl
from jax.experimental.pallas import tpu as pltpu
from jax.sharding import PartitionSpec as P

ENERGIES = 32
TICKS = 2
BLOCK = 128
GROUP = 8


def dot_nt(left, right):
    return lax.dot_general(
        left,
        right,
        (((1,), (1,)), ((), ())),
        precision=lax.Precision.HIGHEST,
        preferred_element_type=jnp.float32,
    )


def across_lanes(tile, lane):
    return jnp.broadcast_to(tile[:, lane : lane + 1], (8, BLOCK))


def across_sublanes(tile, row):
    return jnp.broadcast_to(tile[row : row + 1, :], (8, BLOCK))


def inverse_factor(block):
    tiles = BLOCK // 8
    sub_id = lax.broadcasted_iota(jnp.int32, (8, BLOCK), 0)
    lane_id = lax.broadcasted_iota(jnp.int32, (8, BLOCK), 1)
    a = [block[8 * t : 8 * t + 8, :] for t in range(tiles)]
    e = [(lane_id == sub_id + 8 * t).astype(jnp.float32) for t in range(tiles)]
    out = [jnp.zeros((8, BLOCK), jnp.float32) for _ in range(tiles)]
    for first in range(0, BLOCK, GROUP):
        top, off = first // 8, first % 8
        col = {
            (t, j): across_lanes(a[t], first + j) for t in range(top, tiles) for j in range(GROUP)
        }
        s = {(i, j): across_sublanes(col[top, j], off + i) for i in range(GROUP) for j in range(i + 1)}
        row_a = [across_sublanes(a[top], off + i) for i in range(GROUP)]
        row_e = [across_sublanes(e[top], off + i) for i in range(GROUP)]
        inv = [None] * GROUP
        low = {}
        for i in range(GROUP):
            inv[i] = 1.0 / s[i, i]
            for j in range(i + 1, GROUP):
                low[j, i] = s[j, i] * inv[i]
            for j in range(i + 1, GROUP):
                for q in range(i + 1, j + 1):
                    s[j, q] = s[j, q] - low[j, i] * s[q, i]
                row_a[j] = row_a[j] - low[j, i] * row_a[i]
                row_e[j] = row_e[j] - low[j, i] * row_e[i]
            out[top] = jnp.where(sub_id == off + i, row_e[i] * lax.rsqrt(s[i, i]), out[top])
        up_a = [None] * GROUP
        up_e = [None] * GROUP
        for i in reversed(range(GROUP)):
            up_a[i] = row_a[i] * inv[i]
            up_e[i] = row_e[i] * inv[i]
            for j in range(i + 1, GROUP):
                up_a[i] = up_a[i] - low[j, i] * up_a[j]
                up_e[i] = up_e[i] - low[j, i] * up_e[j]
        for t in range((first + GROUP) // 8, tiles):
            for j in range(GROUP):
                c = col[t, j]
                if t == top:
                    c = jnp.where(sub_id >= off + GROUP, c, 0.0)
                a[t] = a[t] - c * up_a[j]
                e[t] = e[t] - c * up_e[j]
    return jnp.concatenate(out, 0)


def exit_kernel(system_ref, right_ref, left_ref, green_ref, out_ref, work):
    count = work.shape[0]
    rows = system_ref.shape[1]
    col_count = system_ref.shape[0] // count
    per = BLOCK // rows

    def raw(i, j):
        return jnp.concatenate(
            [system_ref[j * col_count + per * i + p] for p in range(per)], 0
        )

    size = count * BLOCK
    for j in range(count):
        for i in range(j, count):
            work[j, i * BLOCK : (i + 1) * BLOCK, :] = 0.5 * (raw(i, j) + raw(j, i).T)
        chunk = jnp.concatenate([right_ref[per * j + p] for p in range(per)], 0)
        work[j, size : size + BLOCK, :] = chunk.T
        work[j, size + BLOCK : size + BLOCK + rows, :] = left_ref[j]
    for k in range(count):
        begin = k * BLOCK
        inverse = inverse_factor(work[k, begin : begin + BLOCK, :])
        panel = dot_nt(work[k, begin + BLOCK :, :], inverse)
        for j in range(k + 1, count):
            lead = (j - k - 1) * BLOCK
            work[j, j * BLOCK :, :] -= dot_nt(panel[lead:], panel[lead : lead + BLOCK])
        work[k, size:, :] = panel[size - begin - BLOCK :]
    total = green_ref[...]
    for k in range(count):
        total -= dot_nt(work[k, size + BLOCK :, :], work[k, size : size + BLOCK, :])
    out_ref[...] = total


def exit_tile_of(system, right, left, green):
    rows = green.shape[0]
    count = left.shape[0]
    return pl.pallas_call(
        exit_kernel,
        out_shape=jax.ShapeDtypeStruct(green.shape, jnp.float32),
        scratch_shapes=[pltpu.VMEM((count, count * BLOCK + BLOCK + rows, BLOCK), jnp.float32)],
        cost_estimate=pl.CostEstimate(
            flops=600_000_000, bytes_accessed=2_000_000, transcendentals=0
        ),
        name="exit_tile",
    )(system, right, left, green)


def contract(left_rows, right_rows):
    return lax.dot_general(
        left_rows, right_rows, (((1,), (1,)), ((), ())), preferred_element_type=jnp.float32
    )


def spread(tile, axes, count):
    copies = jnp.broadcast_to(tile[None], (count,) + tile.shape)
    return lax.all_to_all(copies, axes, 0, 0)


def shifted(block, axis, distance):
    devices = range(lax.axis_size(axis))
    route = [(i - distance, i) for i in devices if i - distance in devices]
    return lax.ppermute(block, axis, route)


def local(amplitudes, state_energies, radii_table, plan, entry_r, fresh_r):
    sec_index = lax.axis_index("sec")
    row_count = lax.axis_size("row")
    col_count = lax.axis_size("col")
    own = amplitudes[0]
    tile = own.shape[1]
    gathered = spread(own, "row", row_count)
    everyone = gathered.transpose(1, 0, 2, 3).reshape(2, row_count * tile, own.shape[2])
    bounds = lax.dynamic_slice_in_dim(radii_table, sec_index, 2)
    sector_width = (bounds[1] - bounds[0]).astype(jnp.float32)
    levels = state_energies[0]

    def greens(period):
        energy = plan[0, period].astype(jnp.float32) / ENERGIES
        weight = 8.0 / (sector_width * (levels - energy))
        scaled = (everyone.astype(jnp.float32) * weight).astype(jnp.bfloat16)
        scaled_own = (own[0].astype(jnp.float32) * weight).astype(jnp.bfloat16)
        paired = own.reshape(2 * tile, own.shape[2])
        return jnp.concatenate(
            [
                contract(scaled[0], paired),
                contract(scaled[1], own[1]),
                contract(everyone[1], scaled_own),
            ],
            1,
        )

    results = []
    boundary = entry_r[0]
    later = [
        lax.psum_scatter(greens(period), "col", scatter_dimension=0, tiled=True)
        for period in range(1, TICKS)
    ]
    partial = greens(0)
    parts = lax.all_to_all(
        partial.reshape(col_count, -1, partial.shape[1]), "col", 0, 0
    )
    blocks = parts.sum(0)
    for period in range(TICKS):
        right = spread(blocks[:, tile : 2 * tile], "col", col_count)
        left = spread(blocks[:, 3 * tile :], "row", row_count)
        system = spread(
            blocks[:, :tile] + boundary, ("row", "col"), row_count * col_count
        )
        exit_tile = exit_tile_of(system, right, left, blocks[:, 2 * tile : 3 * tile])
        results.append(exit_tile)
        if period + 1 < TICKS:
            entering = shifted(exit_tile, "sec", 1)
            boundary = jnp.where(sec_index == 0, fresh_r[period], entering)
            blocks = later[period]
    return jnp.stack(results, 0)[:, None]


def solution(mesh):
    placed = (
        P("sec", None, "row", "col"),
        P("sec", "col"),
        P(),
        P("sec", None),
        P("sec", "col", "row"),
        P(None, "col", "row"),
    )
    return jax.shard_map(
        local, mesh=mesh, in_specs=placed, out_specs=P(None, "sec", "col", "row"), check_vma=False
    )
```

```python
import jax
import jax.numpy as jnp
from jax import lax
from jax.experimental import pallas as pl
from jax.experimental.pallas import tpu as pltpu
from jax.sharding import PartitionSpec as P

ENERGIES = 32
TICKS = 2
BLOCK = 128
GROUP = 8


def dot_nt(left, right):
    return lax.dot_general(
        left,
        right,
        (((1,), (1,)), ((), ())),
        precision=lax.Precision.HIGHEST,
        preferred_element_type=jnp.float32,
    )


def dot_nn(left, right):
    return jnp.dot(
        left, right, precision=lax.Precision.HIGHEST, preferred_element_type=jnp.float32
    )


def dot_tn(left, right):
    return lax.dot_general(
        left,
        right,
        (((0,), (0,)), ((), ())),
        precision=lax.Precision.HIGHEST,
        preferred_element_type=jnp.float32,
    )


def across_lanes(tile, lane):
    return jnp.broadcast_to(tile[:, lane : lane + 1], (8, BLOCK))


def across_sublanes(tile, row):
    return jnp.broadcast_to(tile[row : row + 1, :], (8, BLOCK))


def inverse_factor(block):
    tiles = BLOCK // 8
    sub_id = lax.broadcasted_iota(jnp.int32, (8, BLOCK), 0)
    lane_id = lax.broadcasted_iota(jnp.int32, (8, BLOCK), 1)
    a = [block[8 * t : 8 * t + 8, :] for t in range(tiles)]
    e = [(lane_id == sub_id + 8 * t).astype(jnp.float32) for t in range(tiles)]
    out = [jnp.zeros((8, BLOCK), jnp.float32) for _ in range(tiles)]
    for first in range(0, BLOCK, GROUP):
        top, off = first // 8, first % 8
        col = {
            (t, j): across_lanes(a[t], first + j) for t in range(top, tiles) for j in range(GROUP)
        }
        s = {(i, j): across_sublanes(col[top, j], off + i) for i in range(GROUP) for j in range(i + 1)}
        row_a = [across_sublanes(a[top], off + i) for i in range(GROUP)]
        row_e = [across_sublanes(e[top], off + i) for i in range(GROUP)]
        inv = [None] * GROUP
        low = {}
        for i in range(GROUP):
            inv[i] = 1.0 / s[i, i]
            for j in range(i + 1, GROUP):
                low[j, i] = s[j, i] * inv[i]
            for j in range(i + 1, GROUP):
                for q in range(i + 1, j + 1):
                    s[j, q] = s[j, q] - low[j, i] * s[q, i]
                row_a[j] = row_a[j] - low[j, i] * row_a[i]
                row_e[j] = row_e[j] - low[j, i] * row_e[i]
            out[top] = jnp.where(sub_id == off + i, row_e[i] * lax.rsqrt(s[i, i]), out[top])
        up_a = [None] * GROUP
        up_e = [None] * GROUP
        for i in reversed(range(GROUP)):
            up_a[i] = row_a[i] * inv[i]
            up_e[i] = row_e[i] * inv[i]
            for j in range(i + 1, GROUP):
                up_a[i] = up_a[i] - low[j, i] * up_a[j]
                up_e[i] = up_e[i] - low[j, i] * up_e[j]
        for t in range((first + GROUP) // 8, tiles):
            for j in range(GROUP):
                c = col[t, j]
                if t == top:
                    c = jnp.where(sub_id >= off + GROUP, c, 0.0)
                a[t] = a[t] - c * up_a[j]
                e[t] = e[t] - c * up_e[j]
    return jnp.concatenate(out, 0)


def factor_kernel(system_ref, inverse_ref, work):
    count = work.shape[0]
    rows = system_ref.shape[1]
    col_count = system_ref.shape[0] // count
    per = BLOCK // rows
    size = count * BLOCK

    def raw(i, j):
        return jnp.concatenate([system_ref[j * col_count + per * i + p] for p in range(per)], 0)

    for j in range(count):
        for i in range(j, count):
            work[j, i * BLOCK : (i + 1) * BLOCK, :] = 0.5 * (raw(i, j) + raw(j, i).T)
    for k in range(count):
        begin = k * BLOCK
        end = begin + BLOCK
        inverse = inverse_factor(work[k, begin:end, :])
        if k + 1 < count:
            panel = dot_nt(work[k, end:, :], inverse)
            for j in range(k + 1, count):
                lead = (j - k - 1) * BLOCK
                work[j, j * BLOCK :, :] -= dot_nt(panel[lead:], panel[lead : lead + BLOCK])
            work[k, end:, :] = panel
        for j in range(k):
            total = dot_nn(work[j, begin:end, :], inverse_ref[j * BLOCK : (j + 1) * BLOCK, j * BLOCK : (j + 1) * BLOCK])
            for i in range(j + 1, k):
                total += dot_nn(
                    work[i, begin:end, :],
                    inverse_ref[i * BLOCK : (i + 1) * BLOCK, j * BLOCK : (j + 1) * BLOCK],
                )
            inverse_ref[begin:end, j * BLOCK : (j + 1) * BLOCK] = -dot_nn(inverse, total)
        inverse_ref[begin:end, begin:end] = inverse
        if k + 1 < count:
            inverse_ref[begin:end, end:] = jnp.zeros((BLOCK, size - end), jnp.float32)


def inverse_factor_of(system, count):
    rows = system.shape[1]
    size = count * BLOCK
    return pl.pallas_call(
        factor_kernel,
        out_shape=jax.ShapeDtypeStruct((size, size), jnp.float32),
        scratch_shapes=[pltpu.VMEM((count, size, BLOCK), jnp.float32)],
        cost_estimate=pl.CostEstimate(
            flops=30_000_000_000, bytes_accessed=2_000_000, transcendentals=0
        ),
        name="inverse_factor",
    )(system)


def exit_kernel(inverse_ref, right_ref, left_ref, green_ref, out_ref):
    inverse = inverse_ref[...]
    right = jnp.concatenate([right_ref[p] for p in range(right_ref.shape[0])], 0)
    left = jnp.concatenate([left_ref[p] for p in range(left_ref.shape[0])], 1)
    solved = dot_nn(inverse, right)
    out_ref[...] = green_ref[...] - dot_nn(dot_nt(left, inverse), solved)


def exit_tile_of(inverse, right, left, green):
    return pl.pallas_call(
        exit_kernel,
        out_shape=jax.ShapeDtypeStruct(green.shape, jnp.float32),
        cost_estimate=pl.CostEstimate(
            flops=600_000_000, bytes_accessed=1_500_000, transcendentals=0
        ),
        name="exit_tile",
    )(inverse, right, left, green)


def exit_from_coupling_kernel(place_ref, inverse_ref, coupling_ref, green_ref, out_ref, product):
    inverse = inverse_ref[...]
    rows = coupling_ref.shape[1]
    size = inverse.shape[0]
    col_count = size // rows
    per = BLOCK // rows
    row_index, col_index = place_ref[0], place_ref[1]

    def columns(block):
        start = block * col_count
        return jnp.concatenate([coupling_ref[start + p] for p in range(col_count)], 0)

    right = dot_nn(inverse, columns(row_index))
    left = dot_nn(inverse, columns(col_index // per))
    product[...] = dot_tn(left, right)
    half = pl.multiple_of((col_index % per) * rows, rows)
    out_ref[...] = green_ref[...] - product[pl.ds(half, rows), :]


def exit_tile_from_coupling(place, inverse, coupling, green):
    vmem = pl.BlockSpec(memory_space=pltpu.VMEM)
    return pl.pallas_call(
        exit_from_coupling_kernel,
        out_shape=jax.ShapeDtypeStruct(green.shape, jnp.float32),
        in_specs=[pl.BlockSpec(memory_space=pltpu.SMEM), vmem, vmem, vmem],
        scratch_shapes=[pltpu.VMEM((BLOCK, BLOCK), jnp.float32)],
        cost_estimate=pl.CostEstimate(
            flops=800_000_000, bytes_accessed=2_500_000, transcendentals=0
        ),
        name="exit_tile_from_coupling",
    )(place, inverse, coupling, green)


def contract(left_rows, right_rows):
    return lax.dot_general(
        left_rows, right_rows, (((1,), (1,)), ((), ())), preferred_element_type=jnp.float32
    )


def spread(tile, axes, count):
    copies = jnp.broadcast_to(tile[None], (count,) + tile.shape)
    return lax.all_to_all(copies, axes, 0, 0)


def shifted(block, axis, distance):
    devices = range(lax.axis_size(axis))
    route = [(i - distance, i) for i in devices if i - distance in devices]
    return lax.ppermute(block, axis, route)


def local(amplitudes, state_energies, radii_table, plan, entry_r, fresh_r):
    sec_index = lax.axis_index("sec")
    row_count = lax.axis_size("row")
    col_count = lax.axis_size("col")
    own = amplitudes[0]
    tile = own.shape[1]
    gathered = spread(own, "row", row_count)
    everyone = gathered.transpose(1, 0, 2, 3).reshape(2, row_count * tile, own.shape[2])
    bounds = lax.dynamic_slice_in_dim(radii_table, sec_index, 2)
    sector_width = (bounds[1] - bounds[0]).astype(jnp.float32)
    levels = state_energies[0]
    place = jnp.stack([lax.axis_index("row"), lax.axis_index("col")]).astype(jnp.int32)

    def greens(period):
        energy = plan[0, period].astype(jnp.float32) / ENERGIES
        weight = 8.0 / (sector_width * (levels - energy))
        scaled = (everyone.astype(jnp.float32) * weight).astype(jnp.bfloat16)
        paired = own.reshape(2 * tile, own.shape[2])
        blocks = [contract(scaled[0], paired), contract(scaled[1], own[1])]
        if period == 0:
            scaled_own = (own[0].astype(jnp.float32) * weight).astype(jnp.bfloat16)
            blocks.append(contract(everyone[1], scaled_own))
        full = jnp.concatenate(blocks, 1)
        return full.reshape(col_count, full.shape[0] // col_count, full.shape[1])

    def by_kind(blocks):
        return [blocks[:, i : i + tile] for i in range(0, blocks.shape[1], tile)]

    device_count = row_count * col_count
    results = []
    left_left, left_right, green, crossed = by_kind(
        lax.all_to_all(greens(0), "col", 0, 0).sum(0)
    )
    waiting = [greens(period) for period in range(1, TICKS)]
    boundary = entry_r[0]
    for period in range(TICKS):
        system = spread(left_left + boundary, ("row", "col"), device_count)
        if period == 0:
            left = spread(crossed, "row", row_count)
            system, left, left_right, waiting = lax.optimization_barrier(
                (system, left, left_right, waiting)
            )
            copies = jnp.broadcast_to(left_right[None], (col_count,) + left_right.shape)
            parts = lax.all_to_all(
                jnp.concatenate(waiting + [copies], 2), "col", 0, 0
            )
            inverse = inverse_factor_of(system, row_count)
            exit_tile = exit_tile_of(inverse, parts[:, :, -tile:], left, green)
            summed = parts[:, :, :-tile].sum(0)
            later = [
                by_kind(block) for block in jnp.split(summed, TICKS - 1, axis=1)
            ]
        else:
            system, left_right = lax.optimization_barrier((system, left_right))
            coupling = spread(left_right, ("row", "col"), device_count)
            inverse = inverse_factor_of(system, row_count)
            exit_tile = exit_tile_from_coupling(place, inverse, coupling, green)
        results.append(exit_tile)
        if period + 1 < TICKS:
            entering = shifted(exit_tile, "sec", 1)
            boundary = jnp.where(sec_index == 0, fresh_r[period], entering)
            left_left, left_right, green = later[period]
    return jnp.stack(results, 0)[:, None]


def solution(mesh):
    placed = (
        P("sec", None, "row", "col"),
        P("sec", "col"),
        P(),
        P("sec", None),
        P("sec", "col", "row"),
        P(None, "col", "row"),
    )
    return jax.shard_map(
        local, mesh=mesh, in_specs=placed, out_specs=P(None, "sec", "col", "row"), check_vma=False
    )
```

```python
import jax
import jax.numpy as jnp
from jax import lax
from jax.experimental import pallas as pl
from jax.experimental.pallas import tpu as pltpu
from jax.sharding import PartitionSpec as P

ENERGIES = 32
TICKS = 2
BLOCK = 128
GROUP = 8


def dot_nt(left, right):
    return lax.dot_general(
        left,
        right,
        (((1,), (1,)), ((), ())),
        precision=lax.Precision.HIGHEST,
        preferred_element_type=jnp.float32,
    )


def dot_nn(left, right):
    return jnp.dot(
        left, right, precision=lax.Precision.HIGHEST, preferred_element_type=jnp.float32
    )


def dot_tn(left, right):
    return lax.dot_general(
        left,
        right,
        (((0,), (0,)), ((), ())),
        precision=lax.Precision.HIGHEST,
        preferred_element_type=jnp.float32,
    )


def across_lanes(tile, lane):
    return jnp.broadcast_to(tile[:, lane : lane + 1], (8, BLOCK))


def across_sublanes(tile, row):
    return jnp.broadcast_to(tile[row : row + 1, :], (8, BLOCK))


def sum_pairs(terms):
    terms = list(terms)
    while len(terms) > 1:
        terms = [sum(terms[i : i + 2][1:], terms[i]) for i in range(0, len(terms), 2)]
    return terms[0]


def inverse_factor(block):
    tiles = BLOCK // 8
    sub_id = lax.broadcasted_iota(jnp.int32, (8, BLOCK), 0)
    lane_id = lax.broadcasted_iota(jnp.int32, (8, BLOCK), 1)
    zero = jnp.minimum(jnp.abs(block[0:8, :]), 0.0)
    work = [
        [block[8 * t : 8 * t + 8, :], (lane_id == sub_id + 8 * t).astype(jnp.float32)]
        for t in range(tiles)
    ]
    out = [None] * tiles
    for top in range(tiles):
        col = {
            (t, j): across_lanes(work[t][0], GROUP * top + j)
            for t in range(top, tiles)
            for j in range(GROUP)
        }
        lead = [col[top, j] + zero for j in range(GROUP)]
        s = {(i, j): across_sublanes(lead[j], i) for i in range(GROUP) for j in range(i + 1)}
        row = [[across_sublanes(half, i) for half in work[top]] for i in range(GROUP)]
        inv = [None] * GROUP
        low = {}
        done = jnp.zeros((8, BLOCK), jnp.float32)
        for i in range(GROUP):
            inv[i] = 1.0 / s[i, i]
            for j in range(i + 1, GROUP):
                low[j, i] = s[j, i] * inv[i]
            for j in range(i + 1, GROUP):
                for q in range(i + 1, j + 1):
                    s[j, q] = s[j, q] - low[j, i] * s[q, i]
                row[j] = [x - low[j, i] * y for x, y in zip(row[j], row[i])]
            done = jnp.where(sub_id == i, row[i][1] * lax.rsqrt(s[i, i]), done)
        out[top] = done
        if top + 1 == tiles:
            break
        back = {}
        for i in range(GROUP):
            for j in range(i + 1, GROUP):
                back[j, i] = -(low[j, i] + sum(low[j, q] * back[q, i] for q in range(i + 1, j)))
        scaled = [[x * inv[i] for x in row[i]] for i in range(GROUP)]
        up = [
            [
                sum_pairs(
                    [scaled[i][h]] + [back[j, i] * scaled[j][h] for j in range(i + 1, GROUP)]
                )
                for h in range(2)
            ]
            for i in range(GROUP)
        ]
        for t in range(top + 1, tiles):
            for h in range(2):
                for j in range(GROUP):
                    work[t][h] = work[t][h] - col[t, j] * up[j][h]
    return jnp.concatenate(out, 0)


def factor_kernel(system_ref, inverse_ref, work):
    count = work.shape[0]
    rows = system_ref.shape[1]
    col_count = system_ref.shape[0] // count
    per = BLOCK // rows
    size = count * BLOCK

    def raw(i, j):
        return jnp.concatenate([system_ref[j * col_count + per * i + p] for p in range(per)], 0)

    for j in range(count):
        for i in range(j, count):
            work[j, i * BLOCK : (i + 1) * BLOCK, :] = 0.5 * (raw(i, j) + raw(j, i).T)
    for k in range(count):
        begin = k * BLOCK
        end = begin + BLOCK
        inverse = inverse_factor(work[k, begin:end, :])
        if k + 1 < count:
            panel = dot_nt(work[k, end:, :], inverse)
            for j in range(k + 1, count):
                lead = (j - k - 1) * BLOCK
                work[j, j * BLOCK :, :] -= dot_nt(panel[lead:], panel[lead : lead + BLOCK])
            work[k, end:, :] = panel
        for j in range(k):
            total = dot_nn(work[j, begin:end, :], inverse_ref[j * BLOCK : (j + 1) * BLOCK, j * BLOCK : (j + 1) * BLOCK])
            for i in range(j + 1, k):
                total += dot_nn(
                    work[i, begin:end, :],
                    inverse_ref[i * BLOCK : (i + 1) * BLOCK, j * BLOCK : (j + 1) * BLOCK],
                )
            inverse_ref[begin:end, j * BLOCK : (j + 1) * BLOCK] = -dot_nn(inverse, total)
        inverse_ref[begin:end, begin:end] = inverse
        if k + 1 < count:
            inverse_ref[begin:end, end:] = jnp.zeros((BLOCK, size - end), jnp.float32)


def inverse_factor_of(system, count):
    rows = system.shape[1]
    size = count * BLOCK
    return pl.pallas_call(
        factor_kernel,
        out_shape=jax.ShapeDtypeStruct((size, size), jnp.float32),
        scratch_shapes=[pltpu.VMEM((count, size, BLOCK), jnp.float32)],
        cost_estimate=pl.CostEstimate(
            flops=30_000_000_000, bytes_accessed=2_000_000, transcendentals=0
        ),
        name="inverse_factor",
    )(system)


def exit_kernel(place_ref, inverse_ref, coupling_ref, green_ref, out_ref, product):
    inverse = inverse_ref[...]
    rows = coupling_ref.shape[1]
    size = inverse.shape[0]
    col_count = size // rows
    per = BLOCK // rows
    row_index, col_index = place_ref[0], place_ref[1]

    def columns(block):
        start = block * col_count
        return jnp.concatenate([coupling_ref[start + p] for p in range(col_count)], 0)

    right = dot_nn(inverse, columns(row_index))
    left = dot_nn(inverse, columns(col_index // per))
    product[...] = dot_tn(left, right)
    half = pl.multiple_of((col_index % per) * rows, rows)
    out_ref[...] = green_ref[...] - product[pl.ds(half, rows), :]


def exit_tile_of(place, inverse, coupling, green):
    vmem = pl.BlockSpec(memory_space=pltpu.VMEM)
    return pl.pallas_call(
        exit_kernel,
        out_shape=jax.ShapeDtypeStruct(green.shape, jnp.float32),
        in_specs=[pl.BlockSpec(memory_space=pltpu.SMEM), vmem, vmem, vmem],
        scratch_shapes=[pltpu.VMEM((BLOCK, BLOCK), jnp.float32)],
        cost_estimate=pl.CostEstimate(
            flops=800_000_000, bytes_accessed=2_500_000, transcendentals=0
        ),
        name="exit_tile",
    )(place, inverse, coupling, green)


def contract(left_rows, right_rows):
    return lax.dot_general(
        left_rows, right_rows, (((1,), (1,)), ((), ())), preferred_element_type=jnp.float32
    )


def spread(tile, axes, count):
    copies = jnp.broadcast_to(tile[None], (count,) + tile.shape)
    return lax.all_to_all(copies, axes, 0, 0)


def shifted(block, axis, distance):
    devices = range(lax.axis_size(axis))
    route = [(i - distance, i) for i in devices if i - distance in devices]
    return lax.ppermute(block, axis, route)


def local(amplitudes, state_energies, radii_table, plan, entry_r, fresh_r):
    sec_index = lax.axis_index("sec")
    row_count = lax.axis_size("row")
    col_count = lax.axis_size("col")
    own = amplitudes[0]
    tile = own.shape[1]
    gathered = spread(own, "row", row_count)
    everyone = gathered.transpose(1, 0, 2, 3).reshape(2, row_count * tile, own.shape[2])
    bounds = lax.dynamic_slice_in_dim(radii_table, sec_index, 2)
    sector_width = (bounds[1] - bounds[0]).astype(jnp.float32)
    levels = state_energies[0]
    place = jnp.stack([lax.axis_index("row"), lax.axis_index("col")]).astype(jnp.int32)

    def greens(period):
        energy = plan[0, period].astype(jnp.float32) / ENERGIES
        weight = 8.0 / (sector_width * (levels - energy))
        scaled = (everyone.astype(jnp.float32) * weight).astype(jnp.bfloat16)
        paired = own.reshape(2 * tile, own.shape[2])
        return [contract(scaled[0], paired), contract(scaled[1], own[1])]

    device_count = row_count * col_count
    full = jnp.concatenate([block for period in range(TICKS) for block in greens(period)], 1)
    parts = lax.all_to_all(
        full.reshape(col_count, full.shape[0] // col_count, full.shape[1]), "col", 0, 0
    )
    blocks = parts.sum(0)
    results = []
    boundary = entry_r[0]
    for period in range(TICKS):
        left_left, left_right, green = [
            blocks[:, i * tile : (i + 1) * tile] for i in range(3 * period, 3 * period + 3)
        ]
        system = spread(left_left + boundary, ("row", "col"), device_count)
        system, left_right = lax.optimization_barrier((system, left_right))
        coupling = spread(left_right, ("row", "col"), device_count)
        inverse = inverse_factor_of(system, row_count)
        exit_tile = exit_tile_of(place, inverse, coupling, green)
        results.append(exit_tile)
        if period + 1 < TICKS:
            entering = shifted(exit_tile, "sec", 1)
            boundary = jnp.where(sec_index == 0, fresh_r[period], entering)
    return jnp.stack(results, 0)[:, None]


def solution(mesh):
    placed = (
        P("sec", None, "row", "col"),
        P("sec", "col"),
        P(),
        P("sec", None),
        P("sec", "col", "row"),
        P(None, "col", "row"),
    )
    return jax.shard_map(
        local, mesh=mesh, in_specs=placed, out_specs=P(None, "sec", "col", "row"), check_vma=False
    )
```

```python
import jax
import jax.numpy as jnp
from jax import lax
from jax.experimental import pallas as pl
from jax.experimental.pallas import tpu as pltpu
from jax.sharding import PartitionSpec as P

ENERGIES = 32
TICKS = 2
BLOCK = 128
GROUP = 8


def dot_nt(left, right):
    return lax.dot_general(
        left,
        right,
        (((1,), (1,)), ((), ())),
        precision=lax.Precision.HIGHEST,
        preferred_element_type=jnp.float32,
    )


def dot_nn(left, right):
    return jnp.dot(
        left, right, precision=lax.Precision.HIGHEST, preferred_element_type=jnp.float32
    )


def dot_tn(left, right):
    return lax.dot_general(
        left,
        right,
        (((0,), (0,)), ((), ())),
        precision=lax.Precision.HIGHEST,
        preferred_element_type=jnp.float32,
    )


def across_lanes(tile, lane):
    return jnp.broadcast_to(tile[:, lane : lane + 1], (8, BLOCK))


def across_sublanes(tile, row):
    return jnp.broadcast_to(tile[row : row + 1, :], (8, BLOCK))


def sum_pairs(terms):
    terms = list(terms)
    while len(terms) > 1:
        terms = [sum(terms[i : i + 2][1:], terms[i]) for i in range(0, len(terms), 2)]
    return terms[0]


def inverse_factor(block):
    tiles = BLOCK // 8
    sub_id = lax.broadcasted_iota(jnp.int32, (8, BLOCK), 0)
    lane_id = lax.broadcasted_iota(jnp.int32, (8, BLOCK), 1)
    zero = jnp.minimum(jnp.abs(block[0:8, :]), 0.0)
    work = [
        [block[8 * t : 8 * t + 8, :], (lane_id == sub_id + 8 * t).astype(jnp.float32)]
        for t in range(tiles)
    ]
    out = [None] * tiles
    for top in range(tiles):
        col = {
            (t, j): across_lanes(work[t][0], GROUP * top + j)
            for t in range(top, tiles)
            for j in range(GROUP)
        }
        lead = [col[top, j] + zero for j in range(GROUP)]
        s = {(i, j): across_sublanes(lead[j], i) for i in range(GROUP) for j in range(i + 1)}
        row = [[across_sublanes(half, i) for half in work[top]] for i in range(GROUP)]
        inv = [None] * GROUP
        low = {}
        done = jnp.zeros((8, BLOCK), jnp.float32)
        for i in range(GROUP):
            inv[i] = 1.0 / s[i, i]
            for j in range(i + 1, GROUP):
                low[j, i] = s[j, i] * inv[i]
            for j in range(i + 1, GROUP):
                for q in range(i + 1, j + 1):
                    s[j, q] = s[j, q] - low[j, i] * s[q, i]
                row[j] = [x - low[j, i] * y for x, y in zip(row[j], row[i])]
            done = jnp.where(sub_id == i, row[i][1] * lax.rsqrt(s[i, i]), done)
        out[top] = done
        if top + 1 == tiles:
            break
        back = {}
        for i in range(GROUP):
            for j in range(i + 1, GROUP):
                back[j, i] = -(low[j, i] + sum(low[j, q] * back[q, i] for q in range(i + 1, j)))
        scaled = [[x * inv[i] for x in row[i]] for i in range(GROUP)]
        up = [
            [
                sum_pairs(
                    [scaled[i][h]] + [back[j, i] * scaled[j][h] for j in range(i + 1, GROUP)]
                )
                for h in range(2)
            ]
            for i in range(GROUP)
        ]
        for t in range(top + 1, tiles):
            for h in range(2):
                for j in range(GROUP):
                    work[t][h] = work[t][h] - col[t, j] * up[j][h]
    return jnp.concatenate(out, 0)


def factor_kernel(system_ref, inverse_ref, work):
    count = work.shape[0]
    rows = system_ref.shape[1]
    col_count = system_ref.shape[0] // count
    per = BLOCK // rows
    size = count * BLOCK

    def raw(i, j):
        return jnp.concatenate([system_ref[j * col_count + per * i + p] for p in range(per)], 0)

    for j in range(count):
        for i in range(j, count):
            work[j, i * BLOCK : (i + 1) * BLOCK, :] = 0.5 * (raw(i, j) + raw(j, i).T)
    for k in range(count):
        begin = k * BLOCK
        end = begin + BLOCK
        inverse = inverse_factor(work[k, begin:end, :])
        if k + 1 < count:
            panel = dot_nt(work[k, end:, :], inverse)
            for j in range(k + 1, count):
                lead = (j - k - 1) * BLOCK
                work[j, j * BLOCK :, :] -= dot_nt(panel[lead:], panel[lead : lead + BLOCK])
            work[k, end:, :] = panel
        for j in range(k):
            total = dot_nn(work[j, begin:end, :], inverse_ref[j * BLOCK : (j + 1) * BLOCK, j * BLOCK : (j + 1) * BLOCK])
            for i in range(j + 1, k):
                total += dot_nn(
                    work[i, begin:end, :],
                    inverse_ref[i * BLOCK : (i + 1) * BLOCK, j * BLOCK : (j + 1) * BLOCK],
                )
            inverse_ref[begin:end, j * BLOCK : (j + 1) * BLOCK] = -dot_nn(inverse, total)
        inverse_ref[begin:end, begin:end] = inverse
        if k + 1 < count:
            inverse_ref[begin:end, end:] = jnp.zeros((BLOCK, size - end), jnp.float32)


def inverse_factor_of(system, count):
    rows = system.shape[1]
    size = count * BLOCK
    return pl.pallas_call(
        factor_kernel,
        out_shape=jax.ShapeDtypeStruct((size, size), jnp.float32),
        scratch_shapes=[pltpu.VMEM((count, size, BLOCK), jnp.float32)],
        cost_estimate=pl.CostEstimate(
            flops=30_000_000_000, bytes_accessed=2_000_000, transcendentals=0
        ),
        name="inverse_factor",
    )(system)


def exit_kernel(place_ref, inverse_ref, coupling_ref, green_ref, out_ref, product):
    inverse = inverse_ref[...]
    rows = coupling_ref.shape[1]
    size = inverse.shape[0]
    col_count = size // rows
    per = BLOCK // rows
    row_index, col_index = place_ref[0], place_ref[1]

    def columns(block):
        start = block * col_count
        return jnp.concatenate([coupling_ref[start + p] for p in range(col_count)], 0)

    right = dot_nn(inverse, columns(row_index))
    left = dot_nn(inverse, columns(col_index // per))
    product[...] = dot_tn(left, right)
    half = pl.multiple_of((col_index % per) * rows, rows)
    out_ref[...] = green_ref[...] - product[pl.ds(half, rows), :]


def exit_tile_of(place, inverse, coupling, green):
    vmem = pl.BlockSpec(memory_space=pltpu.VMEM)
    return pl.pallas_call(
        exit_kernel,
        out_shape=jax.ShapeDtypeStruct(green.shape, jnp.float32),
        in_specs=[pl.BlockSpec(memory_space=pltpu.SMEM), vmem, vmem, vmem],
        scratch_shapes=[pltpu.VMEM((BLOCK, BLOCK), jnp.float32)],
        cost_estimate=pl.CostEstimate(
            flops=800_000_000, bytes_accessed=2_500_000, transcendentals=0
        ),
        name="exit_tile",
    )(place, inverse, coupling, green)


def contract(left_rows, right_rows):
    return lax.dot_general(
        left_rows, right_rows, (((1,), (1,)), ((), ())), preferred_element_type=jnp.float32
    )


def spread(tile, axes, count):
    copies = jnp.broadcast_to(tile[None], (count,) + tile.shape)
    return lax.all_to_all(copies, axes, 0, 0)


def around_ring(own, axis):
    count = lax.axis_size(axis)
    if count != 4:
        copies = jnp.broadcast_to(own[None], (count,) + own.shape)
        blocks = lax.all_to_all(copies, axis, 0, 0)
        return jnp.concatenate([blocks[i] for i in range(count)], 1)

    def taken(block, distance):
        return lax.ppermute(block, axis, [((i + distance) % count, i) for i in range(count)])

    tile = own.shape[1]
    half = tile // 2
    after = taken(own, 1)
    before = taken(own, -1)
    upper = taken(after[:, :half], 1)
    lower = taken(before[:, half:], -1)
    me = lax.axis_index(axis)
    everyone = jnp.zeros((own.shape[0], count * tile, own.shape[2]), own.dtype)
    for block, distance, offset in (
        (own, 0, 0),
        (after, 1, 0),
        (before, 3, 0),
        (upper, 2, 0),
        (lower, 2, half),
    ):
        start = (me + distance) % count * tile + offset
        everyone = lax.dynamic_update_slice_in_dim(everyone, block, start, 1)
    return everyone


def shifted(block, axis, distance):
    devices = range(lax.axis_size(axis))
    route = [(i - distance, i) for i in devices if i - distance in devices]
    return lax.ppermute(block, axis, route)


def local(amplitudes, state_energies, radii_table, plan, entry_r, fresh_r):
    sec_index = lax.axis_index("sec")
    row_count = lax.axis_size("row")
    col_count = lax.axis_size("col")
    own = amplitudes[0]
    tile = own.shape[1]
    everyone = around_ring(own, "row")
    bounds = lax.dynamic_slice_in_dim(radii_table, sec_index, 2)
    sector_width = (bounds[1] - bounds[0]).astype(jnp.float32)
    levels = state_energies[0]
    place = jnp.stack([lax.axis_index("row"), lax.axis_index("col")]).astype(jnp.int32)

    def greens(period):
        energy = plan[0, period].astype(jnp.float32) / ENERGIES
        weight = 8.0 / (sector_width * (levels - energy))
        scaled = (everyone.astype(jnp.float32) * weight).astype(jnp.bfloat16)
        paired = own.reshape(2 * tile, own.shape[2])
        return [contract(scaled[0], paired), contract(scaled[1], own[1])]

    device_count = row_count * col_count
    full = jnp.concatenate([block for period in range(TICKS) for block in greens(period)], 1)
    parts = lax.all_to_all(
        full.reshape(col_count, full.shape[0] // col_count, full.shape[1]), "col", 0, 0
    )
    blocks = parts.sum(0)
    results = []
    boundary = entry_r[0]
    for period in range(TICKS):
        left_left, left_right, green = [
            blocks[:, i * tile : (i + 1) * tile] for i in range(3 * period, 3 * period + 3)
        ]
        system = spread(left_left + boundary, ("row", "col"), device_count)
        system, left_right = lax.optimization_barrier((system, left_right))
        coupling = spread(left_right, ("row", "col"), device_count)
        inverse = inverse_factor_of(system, row_count)
        exit_tile = exit_tile_of(place, inverse, coupling, green)
        results.append(exit_tile)
        if period + 1 < TICKS:
            entering = shifted(exit_tile, "sec", 1)
            boundary = jnp.where(sec_index == 0, fresh_r[period], entering)
    return jnp.stack(results, 0)[:, None]


def solution(mesh):
    placed = (
        P("sec", None, "row", "col"),
        P("sec", "col"),
        P(),
        P("sec", None),
        P("sec", "col", "row"),
        P(None, "col", "row"),
    )
    return jax.shard_map(
        local, mesh=mesh, in_specs=placed, out_specs=P(None, "sec", "col", "row"), check_vma=False
    )
```
